512 devices in a mesh: section: 16 (over y, x), rows: 32 (over z, core).
Axes of the slice: x: 4, y: 4, z: 16, core: 2. Of those that a mesh axis runs over, the one named last changes fastest.
Arguments:
- activations: bfloat16 [128, 64, 64, 128], P('section', 'rows'), may hold values from -48 to 48
- first_cache: bfloat16 [2, 64, 64, 128], P(None, 'rows'), may hold values from -4 to 4
- second_cache: bfloat16 [2, 64, 64, 128], P(None, 'rows'), may hold values from -4 to 4
- norm1_scale: float32 [128], replicated, may hold values from 0.1 to 1.9
- norm1_shift: float32 [128], replicated, may hold values from -3 to 3
- conv1_weight: bfloat16 [3, 3, 3, 128, 128], replicated, may hold values from -0.109375 to 0.109375
- conv1_bias: float32 [128], replicated, may hold values from -5 to 5
- norm2_scale: float32 [128], replicated, may hold values from 0.1 to 1.9
- norm2_shift: float32 [128], replicated, may hold values from -3 to 3
- conv2_weight: bfloat16 [3, 3, 3, 128, 128], replicated, may hold values from -0.109375 to 0.109375
- conv2_bias: float32 [128], replicated, may hold values from -3 to 3
Outputs:
- block_output: bfloat16 [128, 64, 64, 128], P('section', 'rows')
The draws below stay inside these ranges and needn't reach their ends.
All inputs are finite; a program needn't handle non-finite values.
Results may differ from the reference program's by a relative error of at most 0.007.
Values may be sent and summed in bfloat16 or wider, within the bound.
A program may use at most 64 MiB of HBM per device.

```python
import math
import jax
import jax.numpy as jnp
from jax import lax

C = 128
GROUPS = 32
SPAN = 8
ROWS_DEV = 2
COLS = 64
FRAMES = 128
ROWS = 64
N_SECTION = 16


def draw_activations(key, part):
    key_base = jax.random.fold_in(key, 11)
    key_values, key_rows, key_cols, key_device, key_flip, key_frames = jax.random.split(key_base, 6)
    shape_full = (FRAMES, ROWS, COLS, C)
    row_scale = jnp.exp(jax.random.uniform(key_rows, (ROWS,), jnp.float32) * math.log(1.78))
    col_scale = jnp.exp(jax.random.uniform(key_cols, (COLS,), jnp.float32) * math.log(3.16))
    device_count = ROWS // ROWS_DEV
    flip_bit = jax.random.randint(key_flip, (), 0, 2)
    parity = ((jnp.arange(device_count, dtype=jnp.int32) + flip_bit) % 2).astype(jnp.float32)
    device_level = jnp.exp(0.5 * math.log(10.0) * (jax.random.uniform(key_device, (device_count,), jnp.float32) + parity))
    device_scale = jnp.repeat(device_level, ROWS_DEV)
    frame_level = jnp.exp(jax.random.uniform(key_frames, (FRAMES,), jnp.float32, math.log(0.5), math.log(2.0)))
    base = jax.random.truncated_normal(key_values, -4.0, 4.0, shape_full, jnp.float32)
    factor = row_scale * device_scale
    return (0.06 * base * factor[None, :, None, None] * col_scale[None, None, :, None] * frame_level[:, None, None, None]).astype(jnp.bfloat16)


def block_levels(own_key, dims, cuts, least, largest):
    level = 1.0
    for axis_at, blocks in cuts:
        steps = jax.random.uniform(jax.random.fold_in(jax.random.fold_in(own_key, 6), axis_at), (blocks,), jnp.float32, least / len(cuts), largest / len(cuts))
        level = level * jnp.repeat(jnp.exp(steps), dims[axis_at] // blocks).reshape((-1,) + (1,) * (len(dims) - 1 - axis_at))
    return level


def scatter_about(rng, extent, scale, reach, shards=(), kind=jnp.bfloat16):
    array = scale * jax.random.normal(rng, extent, jnp.float32)
    if shards:
        array = array * block_levels(rng, extent, shards, -0.22, 0.18)
    return jnp.clip(array, -reach, reach).astype(kind)


def setup_inputs(seed: int = 0) -> dict:
    keys = jax.random.split(jax.random.key(seed), 12)
    return {
        "activations": draw_activations(jax.random.fold_in(keys[11], 71), 0),
        "first_cache": scatter_about(keys[1], (2, ROWS, COLS, C), 0.7, 4.0, ((1, 32),)),
        "second_cache": scatter_about(keys[2], (2, ROWS, COLS, C), 0.7, 4.0, ((1, 32),)),
        "norm1_scale": jnp.clip(1.0 + 0.18 * jax.random.normal(keys[3], (C,), jnp.float32), 0.1, 1.9),
        "norm1_shift": scatter_about(keys[4], (C,), 0.5, 3.0, (), jnp.float32),
        "conv1_weight": scatter_about(keys[5], (3, 3, 3, C, C), (27 * C) ** -0.5, 0.109375),
        "conv1_bias": scatter_about(keys[6], (C,), 1.0, 5.0, (), jnp.float32),
        "norm2_scale": jnp.clip(1.0 + 0.18 * jax.random.normal(keys[7], (C,), jnp.float32), 0.1, 1.9),
        "norm2_shift": scatter_about(keys[8], (C,), 0.5, 3.0, (), jnp.float32),
        "conv2_weight": scatter_about(keys[9], (3, 3, 3, C, C), (27 * C) ** -0.5, 0.109375),
        "conv2_bias": scatter_about(keys[10], (C,), 0.5, 3.0, (), jnp.float32),
    }


epsilon = 1e-06

def norm_silu(values, scale, shift):
    spans = values.reshape(N_SECTION, SPAN, ROWS, COLS, C)

    def per_span(span_block):
        grouped = span_block.astype(jnp.float32).reshape(SPAN, ROWS, COLS, GROUPS, C // GROUPS)
        average = lax.optimization_barrier(jnp.mean(grouped, axis=(0, 1, 2, 4), keepdims=True))
        centred = grouped - average
        spread = lax.optimization_barrier(jnp.mean(centred * centred, axis=(0, 1, 2, 4), keepdims=True))
        normal = (centred / jnp.sqrt(spread + epsilon)).reshape(SPAN, ROWS, COLS, C)
        return jax.nn.silu(normal * scale + shift).astype(jnp.bfloat16)
    return lax.map(per_span, spans).reshape(FRAMES, ROWS, COLS, C)

def causal_conv(source, weight, bias):
    padded = jnp.pad(source, ((0, 0), (1, 1), (1, 1), (0, 0)))

    def per_frame(frame_index):
        window = lax.dynamic_slice_in_dim(padded, frame_index, 3, 0)
        totals = jnp.zeros((ROWS * COLS, C), jnp.float32)
        for frame_tap in range(3):
            for row_tap in range(3):
                for col_tap in range(3):
                    piece = window[frame_tap, row_tap:row_tap + ROWS, col_tap:col_tap + COLS].reshape(ROWS * COLS, C)
                    totals = totals + jnp.dot(piece, weight[frame_tap, row_tap, col_tap], preferred_element_type=jnp.float32)
        return totals.reshape(ROWS, COLS, C)
    return lax.map(per_frame, jnp.arange(FRAMES, dtype=jnp.int32)) + bias

def reference(activations, first_cache, second_cache, norm1_scale, norm1_shift, conv1_weight, conv1_bias, norm2_scale, norm2_shift, conv2_weight, conv2_bias):
    entry_block = norm_silu(activations, norm1_scale, norm1_shift)
    middle = causal_conv(jnp.concatenate([first_cache, entry_block], 0), conv1_weight, conv1_bias).astype(jnp.bfloat16)
    second = norm_silu(middle, norm2_scale, norm2_shift)
    final = causal_conv(jnp.concatenate([second_cache, second], 0), conv2_weight, conv2_bias)
    return (activations.astype(jnp.float32) + final).astype(jnp.bfloat16)
```

```python
import functools

import jax
import jax.numpy as jnp
from jax import lax
from jax.experimental import pallas as pl
from jax.experimental.pallas import tpu as pltpu
from jax.sharding import PartitionSpec as P

MESH = pl.DeviceIdType.MESH
EPS = 1e-06
F32 = jnp.float32
BF16 = jnp.bfloat16
SPAN, ROWS, COLS, C = 8, 2, 64, 128


def lane_group_sum(x):
    lane = lax.broadcasted_iota(jnp.int32, x.shape, 1)
    x = x + jnp.where(lane % 2 == 0, pltpu.roll(x, 127, 1), pltpu.roll(x, 1, 1))
    return x + jnp.where(lane % 4 < 2, pltpu.roll(x, 126, 1), pltpu.roll(x, 2, 1))


def kernel(
    n_sec,
    n_row,
    acts,
    cache1,
    cache2,
    g1,
    b1,
    w1,
    bias1,
    g2,
    b2,
    w2,
    bias2,
    out,
    xa,
    mid,
    par,
    wb1,
    wb2,
    u,
    pb,
    hl,
    hr,
    pv,
    st,
    mv,
    load_sem,
    w_sem,
    halo_send,
    halo_recv,
    cache_send,
    cache_loc,
    st_send,
    st_recv,
    mv_send,
    mv_recv,
):
    s = lax.axis_index("section")
    r = lax.axis_index("rows")
    first, last = s == 0, s == n_sec - 1
    top, bottom = r == 0, r == n_row - 1
    has_up, has_down = jnp.logical_not(top), jnp.logical_not(bottom)
    has_prev, has_next = jnp.logical_not(first), jnp.logical_not(last)
    both = jnp.logical_and

    def dev(ds, dr):
        return {"section": s + ds, "rows": r + dr}

    barrier = pltpu.get_barrier_semaphore()

    def greet(k, carry):
        pl.semaphore_signal(
            barrier, inc=1, device_id={"section": s, "rows": lax.rem(r + k, n_row)}, device_id_type=MESH
        )
        return carry

    lax.fori_loop(1, n_row, greet, 0)
    near = []
    for ds, cs in ((-1, has_prev), (1, has_next)):
        near.append((ds, 0, cs))
        near.append((ds, -1, both(cs, has_up)))
        near.append((ds, 1, both(cs, has_down)))
    expected = jnp.int32(n_row - 1)
    for ds, dr, cond in near:

        @pl.when(cond)
        def _(ds=ds, dr=dr):
            pl.semaphore_signal(barrier, inc=1, device_id=dev(ds, dr), device_id_type=MESH)

        expected = expected + cond.astype(jnp.int32)

    load_x = pltpu.make_async_copy(acts, xa, load_sem.at[0])
    load_x.start()
    par_loads = []
    for i, ref in enumerate((g1, b1, bias1, g2, b2, bias2)):
        par_loads.append(pltpu.make_async_copy(ref, par.at[i], load_sem.at[1 + i]))
        par_loads[-1].start()
    w_loads = []
    for conv, (w, wb) in enumerate(((w1, wb1), (w2, wb2))):
        for dh in range(3):
            for o in range(2):
                rr = dh + o
                copy = pltpu.make_async_copy(
                    w.at[:, dh],
                    wb.at[:, :, rr * C : (rr + 1) * C, o * C : (o + 1) * C],
                    w_sem.at[conv, dh * 2 + o],
                )
                copy.start()
                w_loads.append((conv, copy))
    for wb in (wb1, wb2):
        wb[:, :, 0:C, C : 2 * C] = jnp.zeros((3, 3, C, C), BF16)
        wb[:, :, 3 * C : 4 * C, 0:C] = jnp.zeros((3, 3, C, C), BF16)

    def halo(conv, src):
        out_copies = []

        def add(idx, cond, a, b, ds, dr):
            out_copies.append(
                (
                    cond,
                    pltpu.make_async_remote_copy(
                        src_ref=a,
                        dst_ref=b,
                        send_sem=halo_send.at[conv, idx],
                        recv_sem=halo_recv.at[conv, idx],
                        device_id=dev(ds, dr),
                        device_id_type=MESH,
                    ),
                )
            )

        tail = pl.ds(SPAN - 2, 2)
        add(0, has_down, src.at[:, 1], hl.at[conv], 0, 1)
        add(1, has_up, src.at[:, 0], hr.at[conv], 0, -1)
        add(2, has_next, src.at[tail], pv.at[conv, :, 1:3], 1, 0)
        add(3, both(has_next, has_down), src.at[tail, 1], pv.at[conv, :, 0], 1, 1)
        add(4, both(has_next, has_up), src.at[tail, 0], pv.at[conv, :, 3], 1, -1)
        return out_copies

    def cache_copies(conv, cache):
        local = pltpu.make_async_copy(cache, pv.at[conv, :, 1:3], cache_loc.at[conv])
        remote = []
        for idx, cond, row, slot, dr in ((3, has_down, 1, 0, 1), (4, has_up, 0, 3, -1)):
            remote.append(
                (
                    cond,
                    pltpu.make_async_remote_copy(
                        src_ref=cache.at[:, row],
                        dst_ref=pv.at[conv, :, slot],
                        send_sem=cache_send.at[conv, idx - 3],
                        recv_sem=halo_recv.at[conv, idx],
                        device_id=dev(0, dr),
                        device_id_type=MESH,
                    ),
                )
            )
        return local, remote

    def start_all(copies, extra=None):
        for cond, copy in copies:

            @pl.when(cond if extra is None else both(cond, extra))
            def _(copy=copy):
                copy.start()

    def wait_send_all(copies, extra=None):
        for cond, copy in copies:

            @pl.when(cond if extra is None else both(cond, extra))
            def _(copy=copy):
                copy.wait_send()

    def stat_copy(conv, k):
        peer = lax.rem(r + k, n_row)
        return pltpu.make_async_remote_copy(
            src_ref=st.at[conv, r],
            dst_ref=st.at[conv, r],
            send_sem=st_send.at[conv],
            recv_sem=st_recv.at[conv],
            device_id={"section": s, "rows": peer},
            device_id_type=MESH,
        )

    def local_stats(conv, load):
        x = load()
        mean = jnp.sum(jnp.sum(x, axis=0), axis=0, keepdims=True) * (1.0 / (SPAN * ROWS * COLS))
        d = x - mean[None]
        m2 = jnp.sum(jnp.sum(d * d, axis=0), axis=0, keepdims=True)
        st[conv, r] = jnp.concatenate([mean, m2], axis=0)

        def send(k, carry):
            stat_copy(conv, k).start()
            return carry

        lax.fori_loop(1, n_row, send, 0)

    def wait_stats(conv):
        bulk = st.at[conv, pl.ds(0, n_row - 1)]
        pltpu.make_async_copy(bulk, bulk, st_recv.at[conv]).wait()

    def wait_stats_sent(conv):
        bulk = st.at[conv, pl.ds(0, n_row - 1)]
        pltpu.make_async_copy(bulk, bulk, st_send.at[conv]).wait()

    def combine(conv, scale):
        means = st[conv, :, 0, :]
        m2s = st[conv, :, 1, :]
        total = jnp.sum(means, axis=0, keepdims=True)
        mean = lane_group_sum(jnp.broadcast_to(total, (8, C)))[0:1] * (1.0 / (4 * n_row))
        d = means - mean
        q = jnp.sum(m2s + (SPAN * ROWS * COLS) * (d * d), axis=0, keepdims=True)
        spread = lane_group_sum(jnp.broadcast_to(q, (8, C)))[0:1] * (1.0 / (4 * SPAN * ROWS * COLS * n_row))
        factor = scale / jnp.sqrt(spread + EPS)
        mv[conv, 0] = jnp.concatenate([mean, factor], axis=0)

    def mv_copy(conv):
        return pltpu.make_async_remote_copy(
            src_ref=mv.at[conv, 0],
            dst_ref=mv.at[conv, 1],
            send_sem=mv_send.at[conv],
            recv_sem=mv_recv.at[conv],
            device_id=dev(1, 0),
            device_id_type=MESH,
        )

    def norm(x, mean, factor, shift):
        v = (x.astype(F32) - mean) * factor + shift
        return (v / (1.0 + jnp.exp(-v))).astype(BF16)

    def fill_own(conv, src, shift):
        mean = mv[conv, 0, 0:1, :]
        factor = mv[conv, 0, 1:2, :]

        def own(f, carry):
            for row in range(2):
                u[f + 2, :, (row + 1) * C : (row + 2) * C] = norm(src[f, row], mean, factor, shift)
            return carry

        lax.fori_loop(0, SPAN, own, 0)
        for idx, cond, ref, rr in ((0, has_up, hl, 0), (1, has_down, hr, 3)):

            @pl.when(cond)
            def _(idx=idx, ref=ref, rr=rr):
                pltpu.make_async_copy(ref.at[conv], ref.at[conv], halo_recv.at[conv, idx]).wait()

                def step(f, carry):
                    u[f + 2, :, rr * C : (rr + 1) * C] = norm(ref[conv, f], mean, factor, shift)
                    return carry

                lax.fori_loop(0, SPAN, step, 0)

    def fill_prev(conv, shift):
        @pl.when(has_prev)
        def _():
            pltpu.make_async_copy(mv.at[conv, 1], mv.at[conv, 1], mv_recv.at[conv]).wait()
            pltpu.make_async_copy(pv.at[conv, :, 1:3], pv.at[conv, :, 1:3], halo_recv.at[conv, 2]).wait()

        @pl.when(first)
        def _():
            pltpu.make_async_copy(pv.at[conv, :, 1:3], pv.at[conv, :, 1:3], cache_loc.at[conv]).wait()

        for idx, cond, slot in ((3, has_up, 0), (4, has_down, 3)):

            @pl.when(cond)
            def _(idx=idx, slot=slot):
                pltpu.make_async_copy(pv.at[conv, :, slot], pv.at[conv, :, slot], halo_recv.at[conv, idx]).wait()

        for slot, cond in ((0, has_up), (1, None), (2, None), (3, has_down)):
            lanes = slice(slot * C, (slot + 1) * C)

            @pl.when(has_prev if cond is None else both(cond, has_prev))
            def _(slot=slot, lanes=lanes):
                mean = mv[conv, 1, 0:1, :]
                factor = mv[conv, 1, 1:2, :]
                for f in range(2):
                    u[f, :, lanes] = norm(pv[conv, f, slot], mean, factor, shift)

            @pl.when(first if cond is None else both(cond, first))
            def _(slot=slot, lanes=lanes):
                for f in range(2):
                    u[f, :, lanes] = pv[conv, f, slot]

    def conv_chunk(wb, f0, count):
        m = count * COLS
        lhs = jnp.concatenate([u[f0 + dt : f0 + dt + count].reshape(m, 4 * C) for dt in range(3)], axis=1)
        for dw in range(3):
            rhs = jnp.concatenate([wb[dt, dw] for dt in range(3)], axis=0)
            pb[dw, f0 * COLS : f0 * COLS + m] = jnp.dot(lhs, rhs, preferred_element_type=F32)

    def gathered(f, bias):
        rows = pl.ds(pl.multiple_of(f * COLS, COLS), COLS)
        col = lax.broadcasted_iota(jnp.int32, (COLS, 2 * C), 0)
        low = jnp.where(col == 0, 0.0, pltpu.roll(pb[0, rows], 1, 0))
        high = jnp.where(col == COLS - 1, 0.0, pltpu.roll(pb[2, rows], COLS - 1, 0))
        y = low + pb[1, rows] + high
        return y[:, 0:C] + bias, y[:, C : 2 * C] + bias

    for cond, rr in ((top, 0), (bottom, 3)):

        @pl.when(cond)
        def _(rr=rr):
            u[:, :, rr * C : (rr + 1) * C] = jnp.zeros((SPAN + 2, COLS, C), BF16)

    pl.semaphore_wait(barrier, expected)

    load_x.wait()
    local_stats(0, lambda: xa[...].astype(F32).reshape(SPAN * ROWS, COLS, C))
    halo1 = halo(0, acts)
    start_all(halo1)
    caches = [cache_copies(0, cache1), cache_copies(1, cache2)]
    for local, remote in caches:

        @pl.when(first)
        def _(local=local):
            local.start()

        start_all(remote, first)
    for copy in par_loads:
        copy.wait()
    for conv, copy in w_loads:
        if conv == 0:
            copy.wait()

    wait_stats(0)
    combine(0, par[0:1])
    send_mv = mv_copy(0)

    @pl.when(has_next)
    def _():
        send_mv.start()

    fill_own(0, xa, par[1:2])
    conv_chunk(wb1, 2, SPAN - 2)
    fill_prev(0, par[1:2])
    conv_chunk(wb1, 0, 2)

    def store_mid(f, carry):
        lo, hi = gathered(f, par[2:3])
        mid[f, 0] = lo.astype(BF16)
        mid[f, 1] = hi.astype(BF16)
        return carry

    lax.fori_loop(0, SPAN, store_mid, 0)

    halo2 = halo(1, mid)
    local_stats(1, lambda: mid[...].astype(F32).reshape(SPAN * ROWS, COLS, C))
    start_all(halo2)
    for conv, copy in w_loads:
        if conv == 1:
            copy.wait()
    wait_send_all(halo1)
    for _, remote in caches:
        wait_send_all(remote, first)
    wait_stats_sent(0)

    @pl.when(has_next)
    def _():
        send_mv.wait_send()

    wait_stats(1)
    combine(1, par[3:4])
    send_mv2 = mv_copy(1)

    @pl.when(has_next)
    def _():
        send_mv2.start()

    fill_own(1, mid, par[4:5])
    conv_chunk(wb2, 2, SPAN - 2)
    fill_prev(1, par[4:5])
    conv_chunk(wb2, 0, 2)

    def store_out(f, carry):
        lo, hi = gathered(f, par[5:6])
        out[f, 0] = (xa[f, 0].astype(F32) + lo).astype(BF16)
        out[f, 1] = (xa[f, 1].astype(F32) + hi).astype(BF16)
        return carry

    lax.fori_loop(0, SPAN, store_out, 0)
    wait_send_all(halo2)
    wait_stats_sent(1)

    @pl.when(has_next)
    def _():
        send_mv2.wait_send()


def solution(mesh):
    n_sec, n_row = mesh.shape["section"], mesh.shape["rows"]

    def step(*args):
        any_spec = pl.BlockSpec(memory_space=pl.ANY)
        return pl.pallas_call(
            functools.partial(kernel, n_sec, n_row),
            out_shape=jax.ShapeDtypeStruct((SPAN, ROWS, COLS, C), BF16),
            in_specs=[any_spec] * 11,
            out_specs=pl.BlockSpec(memory_space=pltpu.VMEM),
            scratch_shapes=[
                pltpu.VMEM((SPAN, ROWS, COLS, C), BF16),
                pltpu.VMEM((SPAN, ROWS, COLS, C), BF16),
                pltpu.VMEM((8, C), F32),
                pltpu.VMEM((3, 3, 4 * C, 2 * C), BF16),
                pltpu.VMEM((3, 3, 4 * C, 2 * C), BF16),
                pltpu.VMEM((SPAN + 2, COLS, 4 * C), BF16),
                pltpu.VMEM((3, SPAN * COLS, 2 * C), F32),
                pltpu.VMEM((2, SPAN, COLS, C), BF16),
                pltpu.VMEM((2, SPAN, COLS, C), BF16),
                pltpu.VMEM((2, 2, 4, COLS, C), BF16),
                pltpu.VMEM((2, n_row, 2, C), F32),
                pltpu.VMEM((2, 2, 2, C), F32),
                pltpu.SemaphoreType.DMA((7,)),
                pltpu.SemaphoreType.DMA((2, 6)),
                pltpu.SemaphoreType.DMA((2, 5)),
                pltpu.SemaphoreType.DMA((2, 5)),
                pltpu.SemaphoreType.DMA((2, 2)),
                pltpu.SemaphoreType.DMA((2,)),
                pltpu.SemaphoreType.DMA((2,)),
                pltpu.SemaphoreType.DMA((2,)),
                pltpu.SemaphoreType.DMA((2,)),
                pltpu.SemaphoreType.DMA((2,)),
            ],
            compiler_params=pltpu.CompilerParams(collective_id=0, has_side_effects=True),
        )(*args)

    rep = P()
    tile = P("section", "rows", None, None)
    cache = P(None, "rows", None, None)
    return jax.shard_map(
        step,
        mesh=mesh,
        in_specs=(tile, cache, cache) + (rep,) * 8,
        out_specs=tile,
        check_vma=False,
    )
```

```python
import functools

import jax
import jax.numpy as jnp
from jax import lax
from jax.experimental import pallas as pl
from jax.experimental.pallas import tpu as pltpu
from jax.sharding import PartitionSpec as P

MESH = pl.DeviceIdType.MESH
EPS = 1e-06
F32 = jnp.float32
BF16 = jnp.bfloat16
SPAN, ROWS, COLS, C = 8, 2, 64, 128


def lane_group_sum(x):
    lane = lax.broadcasted_iota(jnp.int32, x.shape, 1)
    x = x + jnp.where(lane % 2 == 0, pltpu.roll(x, 127, 1), pltpu.roll(x, 1, 1))
    return x + jnp.where(lane % 4 < 2, pltpu.roll(x, 126, 1), pltpu.roll(x, 2, 1))


def kernel(
    n_sec,
    n_row,
    acts,
    cache1,
    cache2,
    g1,
    b1,
    w1,
    bias1,
    g2,
    b2,
    w2,
    bias2,
    out,
    xa,
    mid,
    par,
    wb1,
    wb2,
    u,
    pb,
    hl,
    hr,
    pv,
    st,
    mv,
    load_sem,
    w_sem,
    halo_send,
    halo_recv,
    cache_send,
    cache_loc,
    st_send,
    st_recv,
    mv_send,
    mv_recv,
):
    s = lax.axis_index("section")
    r = lax.axis_index("rows")
    first, last = s == 0, s == n_sec - 1
    top, bottom = r == 0, r == n_row - 1
    has_up, has_down = jnp.logical_not(top), jnp.logical_not(bottom)
    has_prev, has_next = jnp.logical_not(first), jnp.logical_not(last)
    both = jnp.logical_and

    def dev(ds, dr):
        return {"section": s + ds, "rows": r + dr}

    load_x = pltpu.make_async_copy(acts, xa, load_sem.at[0])
    load_x.start()

    barrier = pltpu.get_barrier_semaphore()

    def row_peer(k):
        peer = r + k
        return jnp.where(peer >= n_row, peer - n_row, peer)

    def far_first(body):
        half = n_row // 2
        body(row_peer(half))

        def pair(k, carry):
            body(row_peer(half + k))
            body(row_peer(half - k))
            return carry

        lax.fori_loop(1, half, pair, 0)

    def greet(peer):
        pl.semaphore_signal(barrier, inc=1, device_id={"section": s, "rows": peer}, device_id_type=MESH)

    far_first(greet)
    near = []
    for ds, cs in ((-1, has_prev), (1, has_next)):
        near.append((ds, 0, cs))
        near.append((ds, -1, both(cs, has_up)))
        near.append((ds, 1, both(cs, has_down)))
    expected = jnp.int32(n_row - 1)
    for ds, dr, cond in near:

        @pl.when(cond)
        def _(ds=ds, dr=dr):
            pl.semaphore_signal(barrier, inc=1, device_id=dev(ds, dr), device_id_type=MESH)

        expected = expected + cond.astype(jnp.int32)

    par_loads = []
    for i, ref in enumerate((g1, b1, bias1, g2, b2, bias2)):
        par_loads.append(pltpu.make_async_copy(ref, par.at[i], load_sem.at[1 + i]))
        par_loads[-1].start()
    w_loads = []
    for conv, (w, wb) in enumerate(((w1, wb1), (w2, wb2))):
        for dh in range(3):
            for o in range(2):
                rr = dh + o
                copy = pltpu.make_async_copy(
                    w.at[:, dh],
                    wb.at[:, :, rr * C : (rr + 1) * C, o * C : (o + 1) * C],
                    w_sem.at[conv, dh * 2 + o],
                )
                copy.start()
                w_loads.append((conv, copy))

    def halo(conv, src):
        out_copies = []

        def add(idx, cond, a, b, ds, dr):
            out_copies.append(
                (
                    cond,
                    pltpu.make_async_remote_copy(
                        src_ref=a,
                        dst_ref=b,
                        send_sem=halo_send.at[conv, idx],
                        recv_sem=halo_recv.at[conv, idx],
                        device_id=dev(ds, dr),
                        device_id_type=MESH,
                    ),
                )
            )

        tail = pl.ds(SPAN - 2, 2)
        add(0, has_down, src.at[:, 1], hl.at[conv], 0, 1)
        add(1, has_up, src.at[:, 0], hr.at[conv], 0, -1)
        add(2, has_next, src.at[tail], pv.at[conv, :, 1:3], 1, 0)
        add(3, both(has_next, has_down), src.at[tail, 1], pv.at[conv, :, 0], 1, 1)
        add(4, both(has_next, has_up), src.at[tail, 0], pv.at[conv, :, 3], 1, -1)
        return out_copies

    def cache_copies(conv, cache):
        local = pltpu.make_async_copy(cache, pv.at[conv, :, 1:3], cache_loc.at[conv])
        remote = []
        for idx, cond, row, slot, dr in ((3, has_down, 1, 0, 1), (4, has_up, 0, 3, -1)):
            remote.append(
                (
                    cond,
                    pltpu.make_async_remote_copy(
                        src_ref=cache.at[:, row],
                        dst_ref=pv.at[conv, :, slot],
                        send_sem=cache_send.at[conv, idx - 3],
                        recv_sem=halo_recv.at[conv, idx],
                        device_id=dev(0, dr),
                        device_id_type=MESH,
                    ),
                )
            )
        return local, remote

    def start_all(copies, extra=None):
        for cond, copy in copies:

            @pl.when(cond if extra is None else both(cond, extra))
            def _(copy=copy):
                copy.start()

    def wait_send_all(copies, extra=None):
        for cond, copy in copies:

            @pl.when(cond if extra is None else both(cond, extra))
            def _(copy=copy):
                copy.wait_send()

    def stat_copy(conv, peer):
        return pltpu.make_async_remote_copy(
            src_ref=st.at[conv, r],
            dst_ref=st.at[conv, r],
            send_sem=st_send.at[conv],
            recv_sem=st_recv.at[conv],
            device_id={"section": s, "rows": peer},
            device_id_type=MESH,
        )

    n_local = SPAN * ROWS * COLS

    def send_stats(conv, mean, src):
        d = src[...].astype(F32).reshape(SPAN * ROWS, COLS, C) - mean[None]
        m2 = jnp.sum(jnp.sum(d * d, axis=0), axis=0, keepdims=True)
        st[conv, r] = jnp.concatenate([mean, m2], axis=0)
        far_first(lambda peer: stat_copy(conv, peer).start())

    def wait_stats(conv):
        bulk = st.at[conv, pl.ds(0, n_row - 1)]
        pltpu.make_async_copy(bulk, bulk, st_recv.at[conv]).wait()

    def wait_stats_sent(conv):
        bulk = st.at[conv, pl.ds(0, n_row - 1)]
        pltpu.make_async_copy(bulk, bulk, st_send.at[conv]).wait()

    def combine(conv, scale):
        means = st[conv, :, 0, :]
        m2s = st[conv, :, 1, :]
        total = jnp.sum(means, axis=0, keepdims=True)
        mean = lane_group_sum(jnp.broadcast_to(total, (8, C)))[0:1] * (1.0 / (4 * n_row))
        d = means - mean
        q = jnp.sum(m2s + (SPAN * ROWS * COLS) * (d * d), axis=0, keepdims=True)
        spread = lane_group_sum(jnp.broadcast_to(q, (8, C)))[0:1] * (1.0 / (4 * SPAN * ROWS * COLS * n_row))
        factor = 0.5 * scale / jnp.sqrt(spread + EPS)
        mv[conv, 0] = jnp.concatenate([mean, factor], axis=0)

    def mv_copy(conv):
        return pltpu.make_async_remote_copy(
            src_ref=mv.at[conv, 0],
            dst_ref=mv.at[conv, 1],
            send_sem=mv_send.at[conv],
            recv_sem=mv_recv.at[conv],
            device_id=dev(1, 0),
            device_id_type=MESH,
        )

    def norm(x, mean, factor, shift):
        h = (x.astype(F32) - mean) * factor + shift
        return h + h * jnp.tanh(h)

    def wait_halo(conv, idx, ref, cond):
        @pl.when(cond)
        def _():
            pltpu.make_async_copy(ref, ref, halo_recv.at[conv, idx]).wait()

    def fill(conv, src, shift, frames):
        mean = mv[conv, 0, 0:1, :]
        factor = mv[conv, 0, 1:2, :]
        for f in frames:
            for row in range(2):
                u[f + 2, :, (row + 1) * C : (row + 2) * C] = norm(src[f, row], mean, factor, shift).astype(BF16)
            for cond, ref, rr in ((has_up, hl, 0), (has_down, hr, 3)):
                y = jnp.where(cond, norm(ref[conv, f], mean, factor, shift), 0.0)
                u[f + 2, :, rr * C : (rr + 1) * C] = y.astype(BF16)

    def wait_prev(conv):
        @pl.when(has_prev)
        def _():
            pltpu.make_async_copy(mv.at[conv, 1], mv.at[conv, 1], mv_recv.at[conv]).wait()
            pltpu.make_async_copy(pv.at[conv, :, 1:3], pv.at[conv, :, 1:3], halo_recv.at[conv, 2]).wait()

        @pl.when(first)
        def _():
            pltpu.make_async_copy(pv.at[conv, :, 1:3], pv.at[conv, :, 1:3], cache_loc.at[conv]).wait()

        wait_halo(conv, 3, pv.at[conv, :, 0], has_up)
        wait_halo(conv, 4, pv.at[conv, :, 3], has_down)

    def fill_prev(conv, shift):
        mean = mv[conv, 1, 0:1, :]
        factor = mv[conv, 1, 1:2, :]
        for f in range(2):
            for slot, cond in ((0, has_up), (1, None), (2, None), (3, has_down)):
                raw = pv[conv, f, slot]
                y = jnp.where(first, raw.astype(F32), norm(raw, mean, factor, shift))
                if cond is not None:
                    y = jnp.where(cond, y, 0.0)
                u[f, :, slot * C : (slot + 1) * C] = y.astype(BF16)

    half_rows = SPAN // 2 * COLS
    mid_k = 6 * C

    def conv_half(wb, half):
        f0 = half * (SPAN // 2)
        rows = slice(half * half_rows, (half + 1) * half_rows)
        lhs = jnp.concatenate(
            [u[f0 + dt : f0 + dt + SPAN // 2].reshape(half_rows, 4 * C) for dt in range(3)], axis=1
        )
        rhs = [jnp.concatenate([wb[dt, dw] for dt in range(3)], axis=0) for dw in range(3)]
        pb[0, rows] = jnp.dot(lhs, rhs[0], preferred_element_type=F32)
        pb[2, rows] = jnp.dot(lhs, rhs[2], preferred_element_type=F32)
        pb[1, rows] = jnp.dot(lhs[:, :mid_k], rhs[1][:mid_k], preferred_element_type=F32)
        pb[3, rows] = jnp.dot(lhs[:, mid_k:], rhs[1][mid_k:], preferred_element_type=F32)

    def gathered(f, bias):
        rows = slice(f * COLS, (f + 1) * COLS)
        col = lax.broadcasted_iota(jnp.int32, (COLS, 2 * C), 0)
        low = jnp.where(col == 0, 0.0, pltpu.roll(pb[0, rows], 1, 0))
        high = jnp.where(col == COLS - 1, 0.0, pltpu.roll(pb[2, rows], COLS - 1, 0))
        y = (low + pb[1, rows]) + (pb[3, rows] + high)
        return y[:, 0:C] + bias, y[:, C : 2 * C] + bias

    def gather_mid(frames, total):
        for f in frames:
            for row, y in enumerate(gathered(f, par[2:3])):
                y = y.astype(BF16)
                mid[f, row] = y
                total = total + y.astype(F32)
        return total

    def gather_out(frames):
        for f in frames:
            for row, y in enumerate(gathered(f, par[5:6])):
                out[f, row] = (xa[f, row].astype(F32) + y).astype(BF16)

    load_x.wait()
    x = xa[...].astype(F32).reshape(SPAN * ROWS, COLS, C)
    mean = jnp.sum(jnp.sum(x, axis=0), axis=0, keepdims=True) * (1.0 / n_local)
    pl.semaphore_wait(barrier, expected)
    send_stats(0, mean, xa)
    halo1 = halo(0, acts)
    start_all(halo1)
    caches = [cache_copies(0, cache1), cache_copies(1, cache2)]
    for local, remote in caches:

        @pl.when(first)
        def _(local=local):
            local.start()

        start_all(remote, first)
    for wb in (wb1, wb2):
        wb[:, :, 0:C, C : 2 * C] = jnp.zeros((3, 3, C, C), BF16)
        wb[:, :, 3 * C : 4 * C, 0:C] = jnp.zeros((3, 3, C, C), BF16)
    for copy in par_loads:
        copy.wait()
    for conv, copy in w_loads:
        copy.wait()

    early, late = range(2, SPAN), range(2)

    def stage(conv, src, scale, shift):
        wait_stats(conv)
        combine(conv, scale)
        send_mv = mv_copy(conv)

        @pl.when(has_next)
        def _():
            send_mv.start()

        wait_halo(conv, 0, hl.at[conv], has_up)
        wait_halo(conv, 1, hr.at[conv], has_down)
        fill(conv, src, shift, early)
        conv_half((wb1, wb2)[conv], 1)
        fill(conv, src, shift, late)
        wait_prev(conv)
        fill_prev(conv, shift)
        conv_half((wb1, wb2)[conv], 0)
        return send_mv

    send_mv = stage(0, xa, par[0:1], 0.5 * par[1:2])
    total = gather_mid(range(4, SPAN), jnp.zeros((COLS, C), F32))
    total = gather_mid(range(4), total)

    send_stats(1, jnp.sum(total, axis=0, keepdims=True) * (1.0 / n_local), mid)
    halo2 = halo(1, mid)
    start_all(halo2)
    wait_send_all(halo1)
    for _, remote in caches:
        wait_send_all(remote, first)
    wait_stats_sent(0)

    @pl.when(has_next)
    def _():
        send_mv.wait_send()

    send_mv2 = stage(1, mid, par[3:4], 0.5 * par[4:5])
    gather_out(range(4, SPAN))
    gather_out(range(4))
    wait_send_all(halo2)
    wait_stats_sent(1)

    @pl.when(has_next)
    def _():
        send_mv2.wait_send()


def solution(mesh):
    n_sec, n_row = mesh.shape["section"], mesh.shape["rows"]

    def step(*args):
        any_spec = pl.BlockSpec(memory_space=pl.ANY)
        return pl.pallas_call(
            functools.partial(kernel, n_sec, n_row),
            out_shape=jax.ShapeDtypeStruct((SPAN, ROWS, COLS, C), BF16),
            in_specs=[any_spec] * 11,
            out_specs=pl.BlockSpec(memory_space=pltpu.VMEM),
            scratch_shapes=[
                pltpu.VMEM((SPAN, ROWS, COLS, C), BF16),
                pltpu.VMEM((SPAN, ROWS, COLS, C), BF16),
                pltpu.VMEM((8, C), F32),
                pltpu.VMEM((3, 3, 4 * C, 2 * C), BF16),
                pltpu.VMEM((3, 3, 4 * C, 2 * C), BF16),
                pltpu.VMEM((SPAN + 2, COLS, 4 * C), BF16),
                pltpu.VMEM((4, SPAN * COLS, 2 * C), F32),
                pltpu.VMEM((2, SPAN, COLS, C), BF16),
                pltpu.VMEM((2, SPAN, COLS, C), BF16),
                pltpu.VMEM((2, 2, 4, COLS, C), BF16),
                pltpu.VMEM((2, n_row, 2, C), F32),
                pltpu.VMEM((2, 2, 2, C), F32),
                pltpu.SemaphoreType.DMA((7,)),
                pltpu.SemaphoreType.DMA((2, 6)),
                pltpu.SemaphoreType.DMA((2, 5)),
                pltpu.SemaphoreType.DMA((2, 5)),
                pltpu.SemaphoreType.DMA((2, 2)),
                pltpu.SemaphoreType.DMA((2,)),
                pltpu.SemaphoreType.DMA((2,)),
                pltpu.SemaphoreType.DMA((2,)),
                pltpu.SemaphoreType.DMA((2,)),
                pltpu.SemaphoreType.DMA((2,)),
            ],
            compiler_params=pltpu.CompilerParams(collective_id=0, has_side_effects=True),
        )(*args)

    rep = P()
    tile = P("section", "rows", None, None)
    cache = P(None, "rows", None, None)
    return jax.shard_map(
        step,
        mesh=mesh,
        in_specs=(tile, cache, cache) + (rep,) * 8,
        out_specs=tile,
        check_vma=False,
    )
```

```python
import functools

import jax
import jax.numpy as jnp
from jax import lax
from jax.experimental import pallas as pl
from jax.experimental.pallas import tpu as pltpu
from jax.sharding import PartitionSpec as P

MESH = pl.DeviceIdType.MESH
EPS = 1e-06
F32 = jnp.float32
BF16 = jnp.bfloat16
SPAN, ROWS, COLS, C = 8, 2, 64, 128


def lane_group_sum(x):
    lane = lax.broadcasted_iota(jnp.int32, x.shape, 1)
    x = x + jnp.where(lane % 2 == 0, pltpu.roll(x, 127, 1), pltpu.roll(x, 1, 1))
    return x + jnp.where(lane % 4 < 2, pltpu.roll(x, 126, 1), pltpu.roll(x, 2, 1))


def kernel(
    n_sec,
    n_row,
    acts,
    cache1,
    cache2,
    g1,
    b1,
    w1,
    bias1,
    g2,
    b2,
    w2,
    bias2,
    out,
    xa,
    mid,
    par,
    wb1,
    wb2,
    u,
    pb,
    hl,
    hr,
    pv,
    win,
    part,
    full,
    mv,
    load_sem,
    w_sem,
    halo_send,
    halo_recv,
    cache_send,
    cache_loc,
    win_send,
    win_recv,
    part_send,
    part_recv,
    full_send,
    full_recv,
    go,
):
    s = lax.axis_index("section")
    r = lax.axis_index("rows")
    first, last = s == 0, s == n_sec - 1
    top, bottom = r == 0, r == n_row - 1
    has_up, has_down = jnp.logical_not(top), jnp.logical_not(bottom)
    has_prev, has_next = jnp.logical_not(first), jnp.logical_not(last)
    both = jnp.logical_and

    def dev(ds, dr):
        return {"section": s + ds, "rows": r + dr}

    load_x = pltpu.make_async_copy(acts, xa, load_sem.at[0])
    load_x.start()

    ring = n_row // 2
    reach = ring // 4
    chip, core = lax.div(r, 2), lax.rem(r, 2)

    def at_chip(offset, which):
        c = chip + offset
        c = jnp.where(c >= ring, c - ring, jnp.where(c < 0, c + ring, c))
        return c * 2 + which

    def window(body):
        for j in range(reach, 0, -1):
            for offset in (j, -j):
                for which in range(2):
                    body(offset, at_chip(offset, which))
        body(0, chip * 2 + 1 - core)

    barrier = pltpu.get_barrier_semaphore()

    def greet(ds, peer):
        pl.semaphore_signal(
            barrier, inc=1, device_id={"section": s + ds, "rows": peer}, device_id_type=MESH
        )

    window(lambda offset, peer: greet(0, peer))
    for ds, dr, cond in (
        (-1, -1, both(has_prev, has_up)),
        (-1, 0, has_prev),
        (-1, 1, both(has_prev, has_down)),
        (1, 0, has_next),
    ):

        @pl.when(cond)
        def _(ds=ds, dr=dr):
            greet(ds, r + dr)

    expected = jnp.int32(2 * (2 * reach + 1) - 1) + has_prev.astype(jnp.int32)
    for cond in (has_next, both(has_next, has_up), both(has_next, has_down)):
        expected = expected + cond.astype(jnp.int32)

    par_loads = []
    for i, ref in enumerate((g1, b1, bias1, g2, b2, bias2)):
        par_loads.append(pltpu.make_async_copy(ref, par.at[i], load_sem.at[1 + i]))
        par_loads[-1].start()
    w_loads = []
    for conv, (w, wb) in enumerate(((w1, wb1), (w2, wb2))):
        for dh in range(3):
            for o in range(2):
                rr = dh + o
                copy = pltpu.make_async_copy(
                    w.at[:, dh],
                    wb.at[:, :, rr * C : (rr + 1) * C, o * C : (o + 1) * C],
                    w_sem.at[conv, dh * 2 + o],
                )
                copy.start()
                w_loads.append((conv, copy))

    def halo(conv, src):
        out_copies = []

        def add(idx, cond, a, b, ds, dr):
            out_copies.append(
                (
                    cond,
                    pltpu.make_async_remote_copy(
                        src_ref=a,
                        dst_ref=b,
                        send_sem=halo_send.at[conv, idx],
                        recv_sem=halo_recv.at[conv, idx],
                        device_id=dev(ds, dr),
                        device_id_type=MESH,
                    ),
                )
            )

        tail = pl.ds(SPAN - 2, 2)
        add(0, has_down, src.at[:, 1], hl.at[conv], 0, 1)
        add(1, has_up, src.at[:, 0], hr.at[conv], 0, -1)
        add(2, has_next, src.at[tail], pv.at[conv, :, 1:3], 1, 0)
        add(3, both(has_next, has_down), src.at[tail, 1], pv.at[conv, :, 0], 1, 1)
        add(4, both(has_next, has_up), src.at[tail, 0], pv.at[conv, :, 3], 1, -1)
        return out_copies

    def cache_copies(conv, cache):
        local = pltpu.make_async_copy(cache, pv.at[conv, :, 1:3], cache_loc.at[conv])
        remote = []
        for idx, cond, row, slot, dr in ((3, has_down, 1, 0, 1), (4, has_up, 0, 3, -1)):
            remote.append(
                (
                    cond,
                    pltpu.make_async_remote_copy(
                        src_ref=cache.at[:, row],
                        dst_ref=pv.at[conv, :, slot],
                        send_sem=cache_send.at[conv, idx - 3],
                        recv_sem=halo_recv.at[conv, idx],
                        device_id=dev(0, dr),
                        device_id_type=MESH,
                    ),
                )
            )
        return local, remote

    def start_all(copies, extra=None):
        for cond, copy in copies:

            @pl.when(cond if extra is None else both(cond, extra))
            def _(copy=copy):
                copy.start()

    def wait_send_all(copies, extra=None):
        for cond, copy in copies:

            @pl.when(cond if extra is None else both(cond, extra))
            def _(copy=copy):
                copy.wait_send()

    n_local = SPAN * ROWS * COLS
    n_win, n_fwd, n_bwd = 2 * (2 * reach + 1), 2 * reach, 2 * (reach - 1)

    def send(src, dst, send_sem, recv_sem, ds, peer):
        pltpu.make_async_remote_copy(
            src_ref=src,
            dst_ref=dst,
            send_sem=send_sem,
            recv_sem=recv_sem,
            device_id={"section": s + ds, "rows": peer},
            device_id_type=MESH,
        ).start()

    def bulk_wait(ref, sem):
        pltpu.make_async_copy(ref, ref, sem).wait()

    def local_stats(mean, src):
        d = src[...].astype(F32).reshape(SPAN * ROWS, COLS, C) - mean[None]
        m2 = jnp.sum(jnp.sum(d * d, axis=0), axis=0, keepdims=True)
        return jnp.concatenate([mean, m2], axis=0)

    def merged(parts, count, size):
        mean = jnp.sum(parts[:, 0:1, :], axis=0) * (1.0 / count)
        d = parts[:, 0:1, :] - mean[None]
        m2 = jnp.sum(parts[:, 1:2, :] + size * (d * d), axis=0)
        return jnp.concatenate([mean, m2], axis=0)

    def finish(slot, pieces, scale):
        mean = sum(count * jnp.sum(p[:, 0, :], axis=0, keepdims=True) for p, count in pieces)
        mean = lane_group_sum(jnp.broadcast_to(mean, (8, C)))[0:1] * (1.0 / (4 * n_row))
        q = jnp.zeros((1, C), F32)
        for p, count in pieces:
            d = p[:, 0, :] - mean
            q = q + jnp.sum(p[:, 1, :] + (count * n_local) * (d * d), axis=0, keepdims=True)
        spread = lane_group_sum(jnp.broadcast_to(q, (8, C)))[0:1] * (1.0 / (4 * n_local * n_row))
        mv[slot] = jnp.concatenate([mean, 0.5 * scale / jnp.sqrt(spread + EPS)], axis=0)

    def first_exchange(mean):
        mine = 2 * reach + core
        win[mine] = local_stats(mean, xa)
        window(
            lambda offset, peer: send(
                win.at[mine], win.at[2 * (reach - offset) + core], win_send, win_recv, 0, peer
            )
        )

    def second_hop():
        bulk_wait(win.at[pl.ds(0, n_win - 1)], win_recv)
        part[0, 0] = merged(win[...], n_win, n_local)
        part[0, 1] = merged(win[n_win - n_fwd :], n_fwd, n_local)
        if n_bwd:
            part[0, 2] = merged(win[2 : 2 + n_bwd], n_bwd, n_local)
        jobs = [(1, at_chip(-reach, core))]
        if n_bwd:
            jobs.append((2, at_chip(reach, core)))
        for i, peer in jobs:
            send(part.at[0, i], part.at[1, i], part_send.at[0], part_recv.at[0], 0, peer)

        @pl.when(has_next)
        def _():
            pl.semaphore_wait(go.at[0], 1)
            for i, peer in jobs + [(0, r)]:
                send(part.at[0, i], part.at[2, i], part_send.at[1], part_recv.at[1], 1, peer)

        n_jobs = len(jobs)
        bulk_wait(part.at[1, pl.ds(0, n_jobs)], part_recv.at[0])

        @pl.when(has_prev)
        def _():
            pl.semaphore_signal(go.at[1], inc=1, device_id=dev(-1, 0), device_id_type=MESH)

        return n_jobs

    def pieces_of(own):
        out_pieces = [(win[...], 1)] if own else [(part[2, 0:1], n_win)]
        out_pieces.append((part[1 if own else 2, 1:2], n_fwd))
        if n_bwd:
            out_pieces.append((part[1 if own else 2, 2:3], n_bwd))
        return out_pieces

    def second_exchange(mean):
        full[0, r] = local_stats(mean, mid)

        @pl.when(has_next)
        def _():
            pl.semaphore_wait(go.at[1], 1)

        def one(offset):
            peer = r + offset
            peer = jnp.where(peer >= n_row, peer - n_row, peer)
            send(full.at[0, r], full.at[0, r], full_send.at[0], full_recv.at[0], 0, peer)

            @pl.when(has_next)
            def _():
                send(full.at[0, r], full.at[1, r], full_send.at[1], full_recv.at[1], 1, peer)

        half = n_row // 2
        one(half)

        def pair(k, carry):
            one(half + k)
            one(half - k)
            return carry

        lax.fori_loop(1, half, pair, 0)

        @pl.when(has_next)
        def _():
            send(full.at[0, r], full.at[1, r], full_send.at[1], full_recv.at[1], 1, r)

    def norm(x, mean, factor, shift):
        h = (x.astype(F32) - mean) * factor + shift
        return h + h * jnp.tanh(h)

    def wait_halo(conv, idx, ref, cond):
        @pl.when(cond)
        def _():
            pltpu.make_async_copy(ref, ref, halo_recv.at[conv, idx]).wait()

    def fill(conv, src, shift, frames):
        mean = mv[0, 0:1, :]
        factor = mv[0, 1:2, :]
        for f in frames:
            for row in range(2):
                u[f + 2, :, (row + 1) * C : (row + 2) * C] = norm(src[f, row], mean, factor, shift).astype(BF16)
            for cond, ref, rr in ((has_up, hl, 0), (has_down, hr, 3)):
                y = jnp.where(cond, norm(ref[conv, f], mean, factor, shift), 0.0)
                u[f + 2, :, rr * C : (rr + 1) * C] = y.astype(BF16)

    def wait_prev(conv, n_jobs):
        @pl.when(has_prev)
        def _():
            if conv == 0:
                bulk_wait(part.at[2, pl.ds(0, n_jobs + 1)], part_recv.at[1])
            else:
                bulk_wait(full.at[1], full_recv.at[1])
            pltpu.make_async_copy(pv.at[conv, :, 1:3], pv.at[conv, :, 1:3], halo_recv.at[conv, 2]).wait()

        @pl.when(first)
        def _():
            pltpu.make_async_copy(pv.at[conv, :, 1:3], pv.at[conv, :, 1:3], cache_loc.at[conv]).wait()

        wait_halo(conv, 3, pv.at[conv, :, 0], has_up)
        wait_halo(conv, 4, pv.at[conv, :, 3], has_down)

    def fill_prev(conv, shift):
        mean = mv[1, 0:1, :]
        factor = mv[1, 1:2, :]
        for f in range(2):
            for slot, cond in ((0, has_up), (1, None), (2, None), (3, has_down)):
                raw = pv[conv, f, slot]
                y = jnp.where(first, raw.astype(F32), norm(raw, mean, factor, shift))
                if cond is not None:
                    y = jnp.where(cond, y, 0.0)
                u[f, :, slot * C : (slot + 1) * C] = y.astype(BF16)

    half_rows = SPAN // 2 * COLS
    mid_k = 6 * C

    def conv_half(wb, half):
        f0 = half * (SPAN // 2)
        rows = slice(half * half_rows, (half + 1) * half_rows)
        lhs = jnp.concatenate(
            [u[f0 + dt : f0 + dt + SPAN // 2].reshape(half_rows, 4 * C) for dt in range(3)], axis=1
        )
        rhs = [jnp.concatenate([wb[dt, dw] for dt in range(3)], axis=0) for dw in range(3)]
        pb[0, rows] = jnp.dot(lhs, rhs[0], preferred_element_type=F32)
        pb[2, rows] = jnp.dot(lhs, rhs[2], preferred_element_type=F32)
        h = half_rows // 2
        pb[1, half * half_rows : half * half_rows + h] = jnp.dot(lhs[:h], rhs[1], preferred_element_type=F32)
        pb[1, half * half_rows + h : (half + 1) * half_rows] = jnp.dot(lhs[h:], rhs[1], preferred_element_type=F32)

    def gathered(f, bias):
        rows = slice(f * COLS, (f + 1) * COLS)
        col = lax.broadcasted_iota(jnp.int32, (COLS, 2 * C), 0)
        low = jnp.where(col == 0, 0.0, pltpu.roll(pb[0, rows], 1, 0))
        high = jnp.where(col == COLS - 1, 0.0, pltpu.roll(pb[2, rows], COLS - 1, 0))
        y = (low + pb[1, rows]) + high
        return y[:, 0:C] + bias, y[:, C : 2 * C] + bias

    def gather_mid(frames, total):
        for f in frames:
            for row, y in enumerate(gathered(f, par[2:3])):
                y = y.astype(BF16)
                mid[f, row] = y
                total = total + y.astype(F32)
        return total

    def gather_out(frames):
        for f in frames:
            for row, y in enumerate(gathered(f, par[5:6])):
                out[f, row] = (xa[f, row].astype(F32) + y).astype(BF16)

    load_x.wait()
    x = xa[...].astype(F32).reshape(SPAN * ROWS, COLS, C)
    mean = jnp.sum(jnp.sum(x, axis=0), axis=0, keepdims=True) * (1.0 / n_local)
    pl.semaphore_wait(barrier, expected)
    first_exchange(mean)

    @pl.when(has_prev)
    def _():
        pl.semaphore_signal(go.at[0], inc=1, device_id=dev(-1, 0), device_id_type=MESH)

    halo1 = halo(0, acts)
    start_all(halo1)
    caches = [cache_copies(0, cache1), cache_copies(1, cache2)]
    for local, remote in caches:

        @pl.when(first)
        def _(local=local):
            local.start()

        start_all(remote, first)
    for wb in (wb1, wb2):
        wb[:, :, 0:C, C : 2 * C] = jnp.zeros((3, 3, C, C), BF16)
        wb[:, :, 3 * C : 4 * C, 0:C] = jnp.zeros((3, 3, C, C), BF16)
    for copy in par_loads:
        copy.wait()
    for conv, copy in w_loads:
        copy.wait()

    early, late = range(2, SPAN), range(2)

    def stage(conv, src, scale, shift, n_jobs):
        finish(0, pieces_of(True) if conv == 0 else [(full[0], 1)], scale)
        wait_halo(conv, 0, hl.at[conv], has_up)
        wait_halo(conv, 1, hr.at[conv], has_down)
        fill(conv, src, shift, early)
        conv_half((wb1, wb2)[conv], 1)
        fill(conv, src, shift, late)
        wait_prev(conv, n_jobs)
        finish(1, pieces_of(False) if conv == 0 else [(full[1], 1)], scale)
        fill_prev(conv, shift)
        conv_half((wb1, wb2)[conv], 0)

    n_jobs = second_hop()
    stage(0, xa, par[0:1], 0.5 * par[1:2], n_jobs)
    total = gather_mid(range(4, SPAN), jnp.zeros((COLS, C), F32))
    total = gather_mid(range(4), total)

    second_exchange(jnp.sum(total, axis=0, keepdims=True) * (1.0 / n_local))
    halo2 = halo(1, mid)
    start_all(halo2)
    wait_send_all(halo1)
    for _, remote in caches:
        wait_send_all(remote, first)
    bulk_wait(win.at[pl.ds(0, n_win - 1)], win_send)
    bulk_wait(part.at[0, pl.ds(0, n_jobs)], part_send.at[0])

    @pl.when(has_next)
    def _():
        bulk_wait(part.at[0, pl.ds(0, n_jobs + 1)], part_send.at[1])

    bulk_wait(full.at[0, pl.ds(0, n_row - 1)], full_recv.at[0])
    stage(1, mid, par[3:4], 0.5 * par[4:5], n_jobs)
    gather_out(range(4, SPAN))
    gather_out(range(4))
    wait_send_all(halo2)
    bulk_wait(full.at[0, pl.ds(0, n_row - 1)], full_send.at[0])

    @pl.when(has_next)
    def _():
        bulk_wait(full.at[0], full_send.at[1])


def solution(mesh):
    n_sec, n_row = mesh.shape["section"], mesh.shape["rows"]

    def step(*args):
        any_spec = pl.BlockSpec(memory_space=pl.ANY)
        return pl.pallas_call(
            functools.partial(kernel, n_sec, n_row),
            out_shape=jax.ShapeDtypeStruct((SPAN, ROWS, COLS, C), BF16),
            in_specs=[any_spec] * 11,
            out_specs=pl.BlockSpec(memory_space=pltpu.VMEM),
            scratch_shapes=[
                pltpu.VMEM((SPAN, ROWS, COLS, C), BF16),
                pltpu.VMEM((SPAN, ROWS, COLS, C), BF16),
                pltpu.VMEM((8, C), F32),
                pltpu.VMEM((3, 3, 4 * C, 2 * C), BF16),
                pltpu.VMEM((3, 3, 4 * C, 2 * C), BF16),
                pltpu.VMEM((SPAN + 2, COLS, 4 * C), BF16),
                pltpu.VMEM((3, SPAN * COLS, 2 * C), F32),
                pltpu.VMEM((2, SPAN, COLS, C), BF16),
                pltpu.VMEM((2, SPAN, COLS, C), BF16),
                pltpu.VMEM((2, 2, 4, COLS, C), BF16),
                pltpu.VMEM((2 * (2 * (n_row // 8) + 1), 2, C), F32),
                pltpu.VMEM((3, 3, 2, C), F32),
                pltpu.VMEM((2, n_row, 2, C), F32),
                pltpu.VMEM((2, 2, C), F32),
                pltpu.SemaphoreType.DMA((7,)),
                pltpu.SemaphoreType.DMA((2, 6)),
                pltpu.SemaphoreType.DMA((2, 5)),
                pltpu.SemaphoreType.DMA((2, 5)),
                pltpu.SemaphoreType.DMA((2, 2)),
                pltpu.SemaphoreType.DMA((2,)),
                pltpu.SemaphoreType.DMA,
                pltpu.SemaphoreType.DMA,
                pltpu.SemaphoreType.DMA((2,)),
                pltpu.SemaphoreType.DMA((2,)),
                pltpu.SemaphoreType.DMA((2,)),
                pltpu.SemaphoreType.DMA((2,)),
                pltpu.SemaphoreType.REGULAR((2,)),
            ],
            compiler_params=pltpu.CompilerParams(collective_id=0, has_side_effects=True),
        )(*args)

    rep = P()
    tile = P("section", "rows", None, None)
    cache = P(None, "rows", None, None)
    return jax.shard_map(
        step,
        mesh=mesh,
        in_specs=(tile, cache, cache) + (rep,) * 8,
        out_specs=tile,
        check_vma=False,
    )
```

```python
import functools

import jax
import jax.numpy as jnp
from jax import lax
from jax.experimental import pallas as pl
from jax.experimental.pallas import tpu as pltpu
from jax.sharding import PartitionSpec as P

MESH = pl.DeviceIdType.MESH
EPS = 1e-06
F32 = jnp.float32
BF16 = jnp.bfloat16
SPAN, ROWS, COLS, C = 8, 2, 64, 128


def lane_group_sum(x):
    lane = lax.broadcasted_iota(jnp.int32, x.shape, 1)
    x = x + jnp.where(lane % 2 == 0, pltpu.roll(x, 127, 1), pltpu.roll(x, 1, 1))
    return x + jnp.where(lane % 4 < 2, pltpu.roll(x, 126, 1), pltpu.roll(x, 2, 1))


def kernel(
    n_sec,
    n_row,
    acts,
    cache1,
    cache2,
    g1,
    b1,
    w1,
    bias1,
    g2,
    b2,
    w2,
    bias2,
    out,
    xa,
    mid,
    par,
    wb1,
    wb2,
    u,
    pb,
    hl,
    hr,
    pv,
    win,
    part,
    full,
    mv,
    load_sem,
    w_sem,
    halo_send,
    halo_recv,
    cache_send,
    cache_loc,
    win_send,
    win_recv,
    part_send,
    part_recv,
    full_send,
    full_recv,
    go,
):
    s = lax.axis_index("section")
    r = lax.axis_index("rows")
    first, last = s == 0, s == n_sec - 1
    top, bottom = r == 0, r == n_row - 1
    has_up, has_down = jnp.logical_not(top), jnp.logical_not(bottom)
    has_prev, has_next = jnp.logical_not(first), jnp.logical_not(last)
    both = jnp.logical_and

    def dev(ds, dr):
        return {"section": s + ds, "rows": r + dr}

    load_x = pltpu.make_async_copy(acts, xa, load_sem.at[0])
    load_x.start()

    ring = n_row // 2
    reach = ring // 4
    chip, core = lax.div(r, 2), lax.rem(r, 2)

    def at_chip(offset, which):
        c = chip + offset
        c = jnp.where(c >= ring, c - ring, jnp.where(c < 0, c + ring, c))
        return c * 2 + which

    def window(body):
        for j in range(reach, 0, -1):
            for offset in (j, -j):
                for which in range(2):
                    body(offset, at_chip(offset, which))
        body(0, chip * 2 + 1 - core)

    barrier = pltpu.get_barrier_semaphore()

    def greet(ds, peer):
        pl.semaphore_signal(
            barrier, inc=1, device_id={"section": s + ds, "rows": peer}, device_id_type=MESH
        )

    window(lambda offset, peer: greet(0, peer))
    for ds, dr, cond in (
        (-1, -1, both(has_prev, has_up)),
        (-1, 0, has_prev),
        (-1, 1, both(has_prev, has_down)),
        (1, 0, has_next),
    ):

        @pl.when(cond)
        def _(ds=ds, dr=dr):
            greet(ds, r + dr)

    expected = jnp.int32(2 * (2 * reach + 1) - 1) + has_prev.astype(jnp.int32)
    for cond in (has_next, both(has_next, has_up), both(has_next, has_down)):
        expected = expected + cond.astype(jnp.int32)

    par_loads = []
    for i, ref in enumerate((g1, b1, bias1, g2, b2, bias2)):
        par_loads.append(pltpu.make_async_copy(ref, par.at[i], load_sem.at[1 + i]))
        par_loads[-1].start()
    w_loads = []
    for conv, (w, wb) in enumerate(((w1, wb1), (w2, wb2))):
        for dh in range(3):
            for o in range(2):
                rr = dh + o
                copy = pltpu.make_async_copy(
                    w.at[:, dh],
                    wb.at[:, :, rr * C : (rr + 1) * C, o * C : (o + 1) * C],
                    w_sem.at[conv, dh * 2 + o],
                )
                copy.start()
                w_loads.append((conv, copy))

    def halo(conv, src):
        out_copies = []

        def add(idx, cond, a, b, ds, dr):
            out_copies.append(
                (
                    cond,
                    pltpu.make_async_remote_copy(
                        src_ref=a,
                        dst_ref=b,
                        send_sem=halo_send.at[conv, idx],
                        recv_sem=halo_recv.at[conv, idx],
                        device_id=dev(ds, dr),
                        device_id_type=MESH,
                    ),
                )
            )

        tail = pl.ds(SPAN - 2, 2)
        add(0, has_down, src.at[:, 1], hl.at[conv], 0, 1)
        add(1, has_up, src.at[:, 0], hr.at[conv], 0, -1)
        add(2, has_next, src.at[tail], pv.at[conv, :, 1:3], 1, 0)
        add(3, both(has_next, has_down), src.at[tail, 1], pv.at[conv, :, 0], 1, 1)
        add(4, both(has_next, has_up), src.at[tail, 0], pv.at[conv, :, 3], 1, -1)
        return out_copies

    def cache_copies(conv, cache):
        local = pltpu.make_async_copy(cache, pv.at[conv, :, 1:3], cache_loc.at[conv])
        remote = []
        for idx, cond, row, slot, dr in ((3, has_down, 1, 0, 1), (4, has_up, 0, 3, -1)):
            remote.append(
                (
                    cond,
                    pltpu.make_async_remote_copy(
                        src_ref=cache.at[:, row],
                        dst_ref=pv.at[conv, :, slot],
                        send_sem=cache_send.at[conv, idx - 3],
                        recv_sem=halo_recv.at[conv, idx],
                        device_id=dev(0, dr),
                        device_id_type=MESH,
                    ),
                )
            )
        return local, remote

    def start_all(copies, extra=None):
        for cond, copy in copies:

            @pl.when(cond if extra is None else both(cond, extra))
            def _(copy=copy):
                copy.start()

    def wait_send_all(copies, extra=None):
        for cond, copy in copies:

            @pl.when(cond if extra is None else both(cond, extra))
            def _(copy=copy):
                copy.wait_send()

    n_local = SPAN * ROWS * COLS
    n_win, n_fwd, n_bwd = 2 * (2 * reach + 1), 2 * reach, 2 * (reach - 1)

    def send(src, dst, send_sem, recv_sem, ds, peer):
        pltpu.make_async_remote_copy(
            src_ref=src,
            dst_ref=dst,
            send_sem=send_sem,
            recv_sem=recv_sem,
            device_id={"section": s + ds, "rows": peer},
            device_id_type=MESH,
        ).start()

    def bulk_wait(ref, sem):
        pltpu.make_async_copy(ref, ref, sem).wait()

    def local_stats(mean, src):
        d = src[...].astype(F32).reshape(SPAN * ROWS, COLS, C) - mean[None]
        m2 = jnp.sum(jnp.sum(d * d, axis=0), axis=0, keepdims=True)
        return jnp.concatenate([mean, m2], axis=0)

    def merged(parts, count, size):
        mean = jnp.sum(parts[:, 0:1, :], axis=0) * (1.0 / count)
        d = parts[:, 0:1, :] - mean[None]
        m2 = jnp.sum(parts[:, 1:2, :] + size * (d * d), axis=0)
        return jnp.concatenate([mean, m2], axis=0)

    def finish(slot, pieces, scale):
        mean = sum(count * jnp.sum(p[:, 0, :], axis=0, keepdims=True) for p, count in pieces)
        mean = lane_group_sum(jnp.broadcast_to(mean, (8, C)))[0:1] * (1.0 / (4 * n_row))
        q = jnp.zeros((1, C), F32)
        for p, count in pieces:
            d = p[:, 0, :] - mean
            q = q + jnp.sum(p[:, 1, :] + (count * n_local) * (d * d), axis=0, keepdims=True)
        spread = lane_group_sum(jnp.broadcast_to(q, (8, C)))[0:1] * (1.0 / (4 * n_local * n_row))
        mv[slot] = jnp.concatenate([mean, 0.5 * scale / jnp.sqrt(spread + EPS)], axis=0)

    def first_exchange(mean):
        mine = 2 * reach + core
        win[mine] = local_stats(mean, xa)
        window(
            lambda offset, peer: send(
                win.at[mine], win.at[2 * (reach - offset) + core], win_send, win_recv, 0, peer
            )
        )

    def second_hop():
        bulk_wait(win.at[pl.ds(0, n_win - 1)], win_recv)
        part[0, 0] = merged(win[...], n_win, n_local)
        part[0, 1] = merged(win[n_win - n_fwd :], n_fwd, n_local)
        if n_bwd:
            part[0, 2] = merged(win[2 : 2 + n_bwd], n_bwd, n_local)
        jobs = [(1, at_chip(-reach, core))]
        if n_bwd:
            jobs.append((2, at_chip(reach, core)))
        for i, peer in jobs:
            send(part.at[0, i], part.at[1, i], part_send.at[0], part_recv.at[0], 0, peer)

        @pl.when(has_next)
        def _():
            pl.semaphore_wait(go.at[0], 1)
            for i, peer in jobs + [(0, r)]:
                send(part.at[0, i], part.at[2, i], part_send.at[1], part_recv.at[1], 1, peer)

        n_jobs = len(jobs)
        bulk_wait(part.at[1, pl.ds(0, n_jobs)], part_recv.at[0])

        @pl.when(has_prev)
        def _():
            pl.semaphore_signal(go.at[1], inc=1, device_id=dev(-1, 0), device_id_type=MESH)

        return n_jobs

    def pieces_of(own):
        out_pieces = [(win[...], 1)] if own else [(part[2, 0:1], n_win)]
        out_pieces.append((part[1 if own else 2, 1:2], n_fwd))
        if n_bwd:
            out_pieces.append((part[1 if own else 2, 2:3], n_bwd))
        return out_pieces

    def second_exchange(mean):
        full[0, r] = local_stats(mean, mid)

        @pl.when(has_next)
        def _():
            pl.semaphore_wait(go.at[1], 1)

        def one(offset):
            peer = r + offset
            peer = jnp.where(peer >= n_row, peer - n_row, peer)
            send(full.at[0, r], full.at[0, r], full_send.at[0], full_recv.at[0], 0, peer)

            @pl.when(has_next)
            def _():
                send(full.at[0, r], full.at[1, r], full_send.at[1], full_recv.at[1], 1, peer)

        half = n_row // 2
        one(half)

        def pair(k, carry):
            one(half + k)
            one(half - k)
            return carry

        lax.fori_loop(1, half, pair, 0)

        @pl.when(has_next)
        def _():
            send(full.at[0, r], full.at[1, r], full_send.at[1], full_recv.at[1], 1, r)

    def norm(x, mean, factor, shift):
        h = (x.astype(F32) - mean) * factor + shift
        return h + h * jnp.tanh(h)

    def wait_halo(conv, idx, ref, cond):
        @pl.when(cond)
        def _():
            pltpu.make_async_copy(ref, ref, halo_recv.at[conv, idx]).wait()

    def fill(conv, src, shift, frames):
        mean = mv[0, 0:1, :]
        factor = mv[0, 1:2, :]
        for f in frames:
            for row in range(2):
                u[f + 2, :, (row + 1) * C : (row + 2) * C] = norm(src[f, row], mean, factor, shift).astype(BF16)
            for cond, ref, rr in ((has_up, hl, 0), (has_down, hr, 3)):
                y = jnp.where(cond, norm(ref[conv, f], mean, factor, shift), 0.0)
                u[f + 2, :, rr * C : (rr + 1) * C] = y.astype(BF16)

    def wait_prev(conv, n_jobs):
        @pl.when(has_prev)
        def _():
            if conv == 0:
                bulk_wait(part.at[2, pl.ds(0, n_jobs + 1)], part_recv.at[1])
            else:
                bulk_wait(full.at[1], full_recv.at[1])
            pltpu.make_async_copy(pv.at[conv, :, 1:3], pv.at[conv, :, 1:3], halo_recv.at[conv, 2]).wait()

        @pl.when(first)
        def _():
            pltpu.make_async_copy(pv.at[conv, :, 1:3], pv.at[conv, :, 1:3], cache_loc.at[conv]).wait()

        wait_halo(conv, 3, pv.at[conv, :, 0], has_up)
        wait_halo(conv, 4, pv.at[conv, :, 3], has_down)

    def fill_prev(conv, shift):
        mean = mv[1, 0:1, :]
        factor = mv[1, 1:2, :]
        for f in range(2):
            for slot, cond in ((0, has_up), (1, None), (2, None), (3, has_down)):
                raw = pv[conv, f, slot]
                y = jnp.where(first, raw.astype(F32), norm(raw, mean, factor, shift))
                if cond is not None:
                    y = jnp.where(cond, y, 0.0)
                u[f, :, slot * C : (slot + 1) * C] = y.astype(BF16)

    def conv_frames(wb, f0, f1):
        count, mid_row = (f1 - f0) * COLS, (f0 + f1) // 2 * COLS
        lhs = jnp.concatenate([u[f0 + dt : f1 + dt].reshape(count, 4 * C) for dt in range(3)], axis=1)
        rhs = [jnp.concatenate([wb[dt, dw] for dt in range(3)], axis=0) for dw in range(3)]
        lo, hi = f0 * COLS, f1 * COLS
        for dw in (0, 2):
            pb[dw, lo:hi] = jnp.dot(lhs, rhs[dw], preferred_element_type=F32)
        pb[1, lo:mid_row] = jnp.dot(lhs[: mid_row - lo], rhs[1], preferred_element_type=F32)
        pb[1, mid_row:hi] = jnp.dot(lhs[mid_row - lo :], rhs[1], preferred_element_type=F32)

    def gathered(f, bias):
        rows = slice(f * COLS, (f + 1) * COLS)
        col = lax.broadcasted_iota(jnp.int32, (COLS, 2 * C), 0)
        low = jnp.where(col == 0, 0.0, pltpu.roll(pb[0, rows], 1, 0))
        high = jnp.where(col == COLS - 1, 0.0, pltpu.roll(pb[2, rows], COLS - 1, 0))
        y = (low + pb[1, rows]) + high
        return y[:, 0:C] + bias, y[:, C : 2 * C] + bias

    def gather_mid(frames, total):
        for f in frames:
            for row, y in enumerate(gathered(f, par[2:3])):
                y = y.astype(BF16)
                mid[f, row] = y
                total = total + y.astype(F32)
        return total

    def gather_out(frames, carry):
        for f in frames:
            for row, y in enumerate(gathered(f, par[5:6])):
                out[f, row] = (xa[f, row].astype(F32) + y).astype(BF16)

    load_x.wait()
    x = xa[...].astype(F32).reshape(SPAN * ROWS, COLS, C)
    mean = jnp.sum(jnp.sum(x, axis=0), axis=0, keepdims=True) * (1.0 / n_local)
    pl.semaphore_wait(barrier, expected)
    first_exchange(mean)

    @pl.when(has_prev)
    def _():
        pl.semaphore_signal(go.at[0], inc=1, device_id=dev(-1, 0), device_id_type=MESH)

    halo1 = halo(0, acts)
    start_all(halo1)
    caches = [cache_copies(0, cache1), cache_copies(1, cache2)]
    for local, remote in caches:

        @pl.when(first)
        def _(local=local):
            local.start()

        start_all(remote, first)
    for wb in (wb1, wb2):
        wb[:, :, 0:C, C : 2 * C] = jnp.zeros((3, 3, C, C), BF16)
        wb[:, :, 3 * C : 4 * C, 0:C] = jnp.zeros((3, 3, C, C), BF16)
    for copy in par_loads:
        copy.wait()
    for conv, copy in w_loads:
        copy.wait()

    cut = 4

    def stage(conv, src, scale, shift, n_jobs, gather, carry):
        wb = (wb1, wb2)[conv]
        finish(0, pieces_of(True) if conv == 0 else [(full[0], 1)], scale)
        wait_halo(conv, 0, hl.at[conv], has_up)
        wait_halo(conv, 1, hr.at[conv], has_down)
        fill(conv, src, shift, range(cut - 2, SPAN))
        conv_frames(wb, cut, SPAN)
        fill(conv, src, shift, range(cut - 2))
        carry = gather(range(cut, SPAN), carry)
        wait_prev(conv, n_jobs)
        finish(1, pieces_of(False) if conv == 0 else [(full[1], 1)], scale)
        fill_prev(conv, shift)
        conv_frames(wb, 0, cut)
        return gather(range(cut), carry)

    n_jobs = second_hop()
    total = stage(0, xa, par[0:1], 0.5 * par[1:2], n_jobs, gather_mid, jnp.zeros((COLS, C), F32))

    second_exchange(jnp.sum(total, axis=0, keepdims=True) * (1.0 / n_local))
    halo2 = halo(1, mid)
    start_all(halo2)
    wait_send_all(halo1)
    for _, remote in caches:
        wait_send_all(remote, first)
    bulk_wait(win.at[pl.ds(0, n_win - 1)], win_send)
    bulk_wait(part.at[0, pl.ds(0, n_jobs)], part_send.at[0])

    @pl.when(has_next)
    def _():
        bulk_wait(part.at[0, pl.ds(0, n_jobs + 1)], part_send.at[1])

    bulk_wait(full.at[0, pl.ds(0, n_row - 1)], full_recv.at[0])
    stage(1, mid, par[3:4], 0.5 * par[4:5], n_jobs, gather_out, None)
    wait_send_all(halo2)
    bulk_wait(full.at[0, pl.ds(0, n_row - 1)], full_send.at[0])

    @pl.when(has_next)
    def _():
        bulk_wait(full.at[0], full_send.at[1])


def solution(mesh):
    n_sec, n_row = mesh.shape["section"], mesh.shape["rows"]

    def step(*args):
        any_spec = pl.BlockSpec(memory_space=pl.ANY)
        return pl.pallas_call(
            functools.partial(kernel, n_sec, n_row),
            out_shape=pltpu.VMEM((SPAN, ROWS, COLS, C), BF16),
            in_specs=[any_spec] * 11,
            out_specs=pl.BlockSpec(memory_space=pltpu.VMEM),
            scratch_shapes=[
                pltpu.VMEM((SPAN, ROWS, COLS, C), BF16),
                pltpu.VMEM((SPAN, ROWS, COLS, C), BF16),
                pltpu.VMEM((8, C), F32),
                pltpu.VMEM((3, 3, 4 * C, 2 * C), BF16),
                pltpu.VMEM((3, 3, 4 * C, 2 * C), BF16),
                pltpu.VMEM((SPAN + 2, COLS, 4 * C), BF16),
                pltpu.VMEM((3, SPAN * COLS, 2 * C), F32),
                pltpu.VMEM((2, SPAN, COLS, C), BF16),
                pltpu.VMEM((2, SPAN, COLS, C), BF16),
                pltpu.VMEM((2, 2, 4, COLS, C), BF16),
                pltpu.VMEM((2 * (2 * (n_row // 8) + 1), 2, C), F32),
                pltpu.VMEM((3, 3, 2, C), F32),
                pltpu.VMEM((2, n_row, 2, C), F32),
                pltpu.VMEM((2, 2, C), F32),
                pltpu.SemaphoreType.DMA((7,)),
                pltpu.SemaphoreType.DMA((2, 6)),
                pltpu.SemaphoreType.DMA((2, 5)),
                pltpu.SemaphoreType.DMA((2, 5)),
                pltpu.SemaphoreType.DMA((2, 2)),
                pltpu.SemaphoreType.DMA((2,)),
                pltpu.SemaphoreType.DMA,
                pltpu.SemaphoreType.DMA,
                pltpu.SemaphoreType.DMA((2,)),
                pltpu.SemaphoreType.DMA((2,)),
                pltpu.SemaphoreType.DMA((2,)),
                pltpu.SemaphoreType.DMA((2,)),
                pltpu.SemaphoreType.REGULAR((2,)),
            ],
            compiler_params=pltpu.CompilerParams(collective_id=0, has_side_effects=True),
        )(*args)

    rep = P()
    tile = P("section", "rows", None, None)
    cache = P(None, "rows", None, None)
    return jax.shard_map(
        step,
        mesh=mesh,
        in_specs=(tile, cache, cache) + (rep,) * 8,
        out_specs=tile,
        check_vma=False,
    )
```

```python
import functools

import jax
import jax.numpy as jnp
from jax import lax
from jax.experimental import pallas as pl
from jax.experimental.pallas import tpu as pltpu
from jax.sharding import PartitionSpec as P

MESH = pl.DeviceIdType.MESH
EPS = 1e-06
F32 = jnp.float32
BF16 = jnp.bfloat16
SPAN, ROWS, COLS, C = 8, 2, 64, 128


def lane_group_sum(x):
    lane = lax.broadcasted_iota(jnp.int32, x.shape, 1)
    x = x + jnp.where(lane % 2 == 0, pltpu.roll(x, 127, 1), pltpu.roll(x, 1, 1))
    return x + jnp.where(lane % 4 < 2, pltpu.roll(x, 126, 1), pltpu.roll(x, 2, 1))


def kernel(
    n_sec,
    n_row,
    acts,
    cache1,
    cache2,
    g1,
    b1,
    w1,
    bias1,
    g2,
    b2,
    w2,
    bias2,
    out,
    xa,
    mid,
    par,
    wb1,
    wb2,
    u,
    pb,
    hl,
    hr,
    pv,
    win,
    part,
    full,
    mv,
    load_sem,
    w_sem,
    halo_send,
    halo_recv,
    cache_send,
    cache_loc,
    win_send,
    win_recv,
    part_send,
    part_recv,
    full_send,
    full_recv,
    go,
):
    s = lax.axis_index("section")
    r = lax.axis_index("rows")
    first, last = s == 0, s == n_sec - 1
    top, bottom = r == 0, r == n_row - 1
    has_up, has_down = jnp.logical_not(top), jnp.logical_not(bottom)
    has_prev, has_next = jnp.logical_not(first), jnp.logical_not(last)
    both = jnp.logical_and

    def dev(ds, dr):
        return {"section": s + ds, "rows": r + dr}

    load_x = pltpu.make_async_copy(acts, xa, load_sem.at[0])
    load_x.start()

    ring = n_row // 2
    reach = ring // 4
    chip, core = lax.div(r, 2), lax.rem(r, 2)

    def at_chip(offset, which):
        c = chip + offset
        c = jnp.where(c >= ring, c - ring, jnp.where(c < 0, c + ring, c))
        return c * 2 + which

    def window(body):
        for j in range(reach, 0, -1):
            for offset in (j, -j):
                for which in range(2):
                    body(offset, at_chip(offset, which))
        body(0, chip * 2 + 1 - core)

    barrier = pltpu.get_barrier_semaphore()

    def greet(ds, peer):
        pl.semaphore_signal(
            barrier, inc=1, device_id={"section": s + ds, "rows": peer}, device_id_type=MESH
        )

    window(lambda offset, peer: greet(0, peer))
    for ds, dr, cond in (
        (-1, -1, both(has_prev, has_up)),
        (-1, 0, has_prev),
        (-1, 1, both(has_prev, has_down)),
        (1, 0, has_next),
    ):

        @pl.when(cond)
        def _(ds=ds, dr=dr):
            greet(ds, r + dr)

    expected = jnp.int32(2 * (2 * reach + 1) - 1) + has_prev.astype(jnp.int32)
    for cond in (has_next, both(has_next, has_up), both(has_next, has_down)):
        expected = expected + cond.astype(jnp.int32)

    par_loads = []
    for i, ref in enumerate((g1, b1, bias1, g2, b2, bias2)):
        par_loads.append(pltpu.make_async_copy(ref, par.at[i], load_sem.at[1 + i]))
        par_loads[-1].start()
    w_loads = []
    for conv, (w, wb) in enumerate(((w1, wb1), (w2, wb2))):
        for dh in range(3):
            for o in range(2):
                rr = dh + o
                copy = pltpu.make_async_copy(
                    w.at[:, dh],
                    wb.at[:, :, rr * C : (rr + 1) * C, o * C : (o + 1) * C],
                    w_sem.at[conv, dh * 2 + o],
                )
                copy.start()
                w_loads.append((conv, copy))

    def halo(conv, src):
        out_copies = []

        def add(idx, cond, a, b, ds, dr):
            out_copies.append(
                (
                    cond,
                    pltpu.make_async_remote_copy(
                        src_ref=a,
                        dst_ref=b,
                        send_sem=halo_send.at[conv, idx],
                        recv_sem=halo_recv.at[conv, idx],
                        device_id=dev(ds, dr),
                        device_id_type=MESH,
                    ),
                )
            )

        tail = pl.ds(SPAN - 2, 2)
        add(0, has_down, src.at[:, 1], hl.at[conv], 0, 1)
        add(1, has_up, src.at[:, 0], hr.at[conv], 0, -1)
        add(2, has_next, src.at[tail], pv.at[conv, :, 1:3], 1, 0)
        add(3, both(has_next, has_down), src.at[tail, 1], pv.at[conv, :, 0], 1, 1)
        add(4, both(has_next, has_up), src.at[tail, 0], pv.at[conv, :, 3], 1, -1)
        return out_copies

    def cache_copies(conv, cache):
        local = pltpu.make_async_copy(cache, pv.at[conv, :, 1:3], cache_loc.at[conv])
        remote = []
        for idx, cond, row, slot, dr in ((3, has_down, 1, 0, 1), (4, has_up, 0, 3, -1)):
            remote.append(
                (
                    cond,
                    pltpu.make_async_remote_copy(
                        src_ref=cache.at[:, row],
                        dst_ref=pv.at[conv, :, slot],
                        send_sem=cache_send.at[conv, idx - 3],
                        recv_sem=halo_recv.at[conv, idx],
                        device_id=dev(0, dr),
                        device_id_type=MESH,
                    ),
                )
            )
        return local, remote

    def start_all(copies, extra=None):
        for cond, copy in copies:

            @pl.when(cond if extra is None else both(cond, extra))
            def _(copy=copy):
                copy.start()

    def wait_send_all(copies, extra=None):
        for cond, copy in copies:

            @pl.when(cond if extra is None else both(cond, extra))
            def _(copy=copy):
                copy.wait_send()

    n_local = SPAN * ROWS * COLS
    n_win, n_fwd, n_bwd = 2 * (2 * reach + 1), 2 * reach, 2 * (reach - 1)

    def send(src, dst, send_sem, recv_sem, ds, peer):
        pltpu.make_async_remote_copy(
            src_ref=src,
            dst_ref=dst,
            send_sem=send_sem,
            recv_sem=recv_sem,
            device_id={"section": s + ds, "rows": peer},
            device_id_type=MESH,
        ).start()

    def bulk_wait(ref, sem):
        pltpu.make_async_copy(ref, ref, sem).wait()

    def local_stats(mean, src):
        totals = [jnp.zeros((COLS, C), F32), jnp.zeros((COLS, C), F32)]
        for f in range(SPAN):
            for row in range(ROWS):
                d = src[f, row].astype(F32) - mean
                totals[row] = totals[row] + d * d
        m2 = jnp.sum(totals[0] + totals[1], axis=0, keepdims=True)
        return jnp.concatenate([mean, m2], axis=0)

    def merged(parts, count, size):
        mean = jnp.sum(parts[:, 0:1, :], axis=0) * (1.0 / count)
        d = parts[:, 0:1, :] - mean[None]
        m2 = jnp.sum(parts[:, 1:2, :] + size * (d * d), axis=0)
        return jnp.concatenate([mean, m2], axis=0)

    def finish(slot, pieces, scale):
        mean = sum(count * jnp.sum(p[:, 0, :], axis=0, keepdims=True) for p, count in pieces)
        mean = lane_group_sum(jnp.broadcast_to(mean, (8, C)))[0:1] * (1.0 / (4 * n_row))
        q = jnp.zeros((1, C), F32)
        for p, count in pieces:
            d = p[:, 0, :] - mean
            q = q + jnp.sum(p[:, 1, :] + (count * n_local) * (d * d), axis=0, keepdims=True)
        spread = lane_group_sum(jnp.broadcast_to(q, (8, C)))[0:1] * (1.0 / (4 * n_local * n_row))
        mv[slot] = jnp.concatenate([mean, 0.5 * scale / jnp.sqrt(spread + EPS)], axis=0)

    mine = 2 * reach + core

    def first_exchange():
        window(
            lambda offset, peer: send(
                win.at[mine], win.at[2 * (reach - offset) + core], win_send, win_recv, 0, peer
            )
        )

    def second_hop():
        bulk_wait(win.at[pl.ds(0, n_win - 1)], win_recv)
        part[0, 1] = merged(win[n_win - n_fwd :], n_fwd, n_local)
        if n_bwd:
            part[0, 2] = merged(win[2 : 2 + n_bwd], n_bwd, n_local)
        jobs = [(1, at_chip(-reach, core))]
        if n_bwd:
            jobs.append((2, at_chip(reach, core)))
        for i, peer in jobs:
            send(part.at[0, i], part.at[1, i], part_send.at[0], part_recv.at[0], 0, peer)
        part[0, 0] = merged(win[...], n_win, n_local)

        @pl.when(has_next)
        def _():
            pl.semaphore_wait(go.at[0], 1)
            for i, peer in jobs + [(0, r)]:
                send(part.at[0, i], part.at[2, i], part_send.at[1], part_recv.at[1], 1, peer)

        n_jobs = len(jobs)
        bulk_wait(part.at[1, pl.ds(0, n_jobs)], part_recv.at[0])

        @pl.when(has_prev)
        def _():
            pl.semaphore_signal(go.at[1], inc=1, device_id=dev(-1, 0), device_id_type=MESH)

        return n_jobs

    def pieces_of(own):
        out_pieces = [(win[...], 1)] if own else [(part[2, 0:1], n_win)]
        out_pieces.append((part[1 if own else 2, 1:2], n_fwd))
        if n_bwd:
            out_pieces.append((part[1 if own else 2, 2:3], n_bwd))
        return out_pieces

    def second_exchange(mean):
        full[0, r] = local_stats(mean, mid)

        @pl.when(has_next)
        def _():
            pl.semaphore_wait(go.at[1], 1)

        def one(offset):
            peer = r + offset
            peer = jnp.where(peer >= n_row, peer - n_row, peer)
            @pl.when(has_next)
            def _():
                send(full.at[0, r], full.at[1, r], full_send.at[1], full_recv.at[1], 1, peer)

            send(full.at[0, r], full.at[0, r], full_send.at[0], full_recv.at[0], 0, peer)

        half = n_row // 2
        one(half)

        def pair(k, carry):
            one(half + k)
            one(half - k)
            return carry

        lax.fori_loop(1, half, pair, 0)

        @pl.when(has_next)
        def _():
            send(full.at[0, r], full.at[1, r], full_send.at[1], full_recv.at[1], 1, r)

    def norm(x, mean, factor, shift):
        h = (x.astype(F32) - mean) * factor + shift
        return h + h * jnp.tanh(h)

    def wait_halo(conv, idx, ref, cond):
        @pl.when(cond)
        def _():
            pltpu.make_async_copy(ref, ref, halo_recv.at[conv, idx]).wait()

    def fill(conv, src, shift, frames):
        mean = mv[0, 0:1, :]
        factor = mv[0, 1:2, :]
        for f in frames:
            for row in range(2):
                u[f + 2, :, (row + 1) * C : (row + 2) * C] = norm(src[f, row], mean, factor, shift).astype(BF16)
            for cond, ref, rr in ((has_up, hl, 0), (has_down, hr, 3)):
                y = jnp.where(cond, norm(ref[conv, f], mean, factor, shift), 0.0)
                u[f + 2, :, rr * C : (rr + 1) * C] = y.astype(BF16)

    def wait_prev(conv, n_jobs):
        @pl.when(has_prev)
        def _():
            if conv == 0:
                bulk_wait(part.at[2, pl.ds(0, n_jobs + 1)], part_recv.at[1])
            else:
                bulk_wait(full.at[1], full_recv.at[1])
            pltpu.make_async_copy(pv.at[conv, :, 1:3], pv.at[conv, :, 1:3], halo_recv.at[conv, 2]).wait()

        @pl.when(first)
        def _():
            pltpu.make_async_copy(pv.at[conv, :, 1:3], pv.at[conv, :, 1:3], cache_loc.at[conv]).wait()

        wait_halo(conv, 3, pv.at[conv, :, 0], has_up)
        wait_halo(conv, 4, pv.at[conv, :, 3], has_down)

    def fill_prev(conv, shift):
        mean = mv[1, 0:1, :]
        factor = mv[1, 1:2, :]
        for f in range(2):
            for slot, cond in ((0, has_up), (1, None), (2, None), (3, has_down)):
                raw = pv[conv, f, slot]
                y = jnp.where(first, raw.astype(F32), norm(raw, mean, factor, shift))
                if cond is not None:
                    y = jnp.where(cond, y, 0.0)
                u[f, :, slot * C : (slot + 1) * C] = y.astype(BF16)

    def conv_frames(wb, f0, f1):
        lo, hi = f0 * COLS, f1 * COLS
        shape = (hi - lo, 2 * C)
        pl.run_scoped(
            functools.partial(conv_scoped, wb, f0, f1),
            pltpu.ACC(0)(shape, F32),
            pltpu.ACC(0)(shape, F32),
            pltpu.ACC(1)(shape, F32),
            pltpu.ACC(1)(shape, F32),
        )

    def conv_scoped(wb, f0, f1, acc0, acc1, acc2, acc3):
        lo, hi = f0 * COLS, f1 * COLS
        deep = 2 * C

        def lhs_tile(k):
            dt, lane = k // 2, k % 2 * deep
            return u[f0 + dt : f1 + dt, :, lane : lane + deep].reshape(hi - lo, deep)

        def rhs_tile(dw, k):
            dt, row = k // 2, k % 2 * deep
            return wb[dt, dw, row : row + deep, :]

        plans = (
            [(acc0, 0, k) for k in range(6)] + [(acc1, 1, k) for k in range(3)],
            [(acc2, 2, k) for k in range(6)] + [(acc3, 1, k) for k in range(3, 6)],
        )
        for i in range(9):
            for mxu, plan in enumerate(plans):
                acc, dw, k = plan[i]
                pltpu.matmul_push_rhs(rhs_tile(dw, k), i % 2, mxu)
                pltpu.matmul_acc_lhs(acc, lhs_tile(k), load_staged_rhs=i % 2)
        for slot, acc in ((0, acc0), (2, acc2), (1, acc1), (3, acc3)):
            pb[slot, lo:hi] = pltpu.matmul_pop(acc)

    def gathered(f, bias):
        rows = slice(f * COLS, (f + 1) * COLS)
        col = lax.broadcasted_iota(jnp.int32, (COLS, 2 * C), 0)
        low = jnp.where(col == 0, 0.0, pltpu.roll(pb[0, rows], 1, 0))
        high = jnp.where(col == COLS - 1, 0.0, pltpu.roll(pb[2, rows], COLS - 1, 0))
        y = (low + pb[1, rows]) + (pb[3, rows] + high)
        return y[:, 0:C] + bias, y[:, C : 2 * C] + bias

    def gather_mid(frames, total):
        for f in frames:
            for row, y in enumerate(gathered(f, par[2:3])):
                y = y.astype(BF16)
                mid[f, row] = y
                total = total + y.astype(F32)
        return total

    def gather_out(frames, carry):
        for f in frames:
            for row, y in enumerate(gathered(f, par[5:6])):
                out[f, row] = (xa[f, row].astype(F32) + y).astype(BF16)

    load_x.wait()
    x = xa[...].astype(F32).reshape(SPAN * ROWS, COLS, C)
    mean = jnp.sum(jnp.sum(x, axis=0), axis=0, keepdims=True) * (1.0 / n_local)
    win[mine] = local_stats(mean, xa)
    pl.semaphore_wait(barrier, expected)
    first_exchange()

    @pl.when(has_prev)
    def _():
        pl.semaphore_signal(go.at[0], inc=1, device_id=dev(-1, 0), device_id_type=MESH)

    halo1 = halo(0, acts)
    start_all(halo1)
    caches = [cache_copies(0, cache1), cache_copies(1, cache2)]
    for local, remote in caches:

        @pl.when(first)
        def _(local=local):
            local.start()

        start_all(remote, first)
    for wb in (wb1, wb2):
        wb[:, :, 0:C, C : 2 * C] = jnp.zeros((3, 3, C, C), BF16)
        wb[:, :, 3 * C : 4 * C, 0:C] = jnp.zeros((3, 3, C, C), BF16)
    for copy in par_loads:
        copy.wait()
    for conv, copy in w_loads:
        copy.wait()

    cut = 4

    def stage(conv, src, scale, shift, n_jobs, gather, carry):
        wb = (wb1, wb2)[conv]
        finish(0, pieces_of(True) if conv == 0 else [(full[0], 1)], scale)
        wait_halo(conv, 0, hl.at[conv], has_up)
        wait_halo(conv, 1, hr.at[conv], has_down)
        fill(conv, src, shift, range(cut - 2, SPAN))
        conv_frames(wb, cut, SPAN)
        fill(conv, src, shift, range(cut - 2))
        carry = gather(range(cut, SPAN), carry)
        wait_prev(conv, n_jobs)
        finish(1, pieces_of(False) if conv == 0 else [(full[1], 1)], scale)
        fill_prev(conv, shift)
        conv_frames(wb, 0, cut)
        return gather(range(cut), carry)

    n_jobs = second_hop()
    total = stage(0, xa, par[0:1], 0.5 * par[1:2], n_jobs, gather_mid, jnp.zeros((COLS, C), F32))

    second_exchange(jnp.sum(total, axis=0, keepdims=True) * (1.0 / n_local))
    halo2 = halo(1, mid)
    start_all(halo2)
    wait_send_all(halo1)
    for _, remote in caches:
        wait_send_all(remote, first)
    bulk_wait(win.at[pl.ds(0, n_win - 1)], win_send)
    bulk_wait(part.at[0, pl.ds(0, n_jobs)], part_send.at[0])

    @pl.when(has_next)
    def _():
        bulk_wait(part.at[0, pl.ds(0, n_jobs + 1)], part_send.at[1])

    bulk_wait(full.at[0, pl.ds(0, n_row - 1)], full_recv.at[0])
    stage(1, mid, par[3:4], 0.5 * par[4:5], n_jobs, gather_out, None)
    wait_send_all(halo2)
    bulk_wait(full.at[0, pl.ds(0, n_row - 1)], full_send.at[0])

    @pl.when(has_next)
    def _():
        bulk_wait(full.at[0], full_send.at[1])


def solution(mesh):
    n_sec, n_row = mesh.shape["section"], mesh.shape["rows"]

    def step(*args):
        any_spec = pl.BlockSpec(memory_space=pl.ANY)
        return pl.pallas_call(
            functools.partial(kernel, n_sec, n_row),
            out_shape=pltpu.VMEM((SPAN, ROWS, COLS, C), BF16),
            in_specs=[any_spec] * 11,
            out_specs=pl.BlockSpec(memory_space=pltpu.VMEM),
            scratch_shapes=[
                pltpu.VMEM((SPAN, ROWS, COLS, C), BF16),
                pltpu.VMEM((SPAN, ROWS, COLS, C), BF16),
                pltpu.VMEM((8, C), F32),
                pltpu.VMEM((3, 3, 4 * C, 2 * C), BF16),
                pltpu.VMEM((3, 3, 4 * C, 2 * C), BF16),
                pltpu.VMEM((SPAN + 2, COLS, 4 * C), BF16),
                pltpu.VMEM((4, SPAN * COLS, 2 * C), F32),
                pltpu.VMEM((2, SPAN, COLS, C), BF16),
                pltpu.VMEM((2, SPAN, COLS, C), BF16),
                pltpu.VMEM((2, 2, 4, COLS, C), BF16),
                pltpu.VMEM((2 * (2 * (n_row // 8) + 1), 2, C), F32),
                pltpu.VMEM((3, 3, 2, C), F32),
                pltpu.VMEM((2, n_row, 2, C), F32),
                pltpu.VMEM((2, 2, C), F32),
                pltpu.SemaphoreType.DMA((7,)),
                pltpu.SemaphoreType.DMA((2, 6)),
                pltpu.SemaphoreType.DMA((2, 5)),
                pltpu.SemaphoreType.DMA((2, 5)),
                pltpu.SemaphoreType.DMA((2, 2)),
                pltpu.SemaphoreType.DMA((2,)),
                pltpu.SemaphoreType.DMA,
                pltpu.SemaphoreType.DMA,
                pltpu.SemaphoreType.DMA((2,)),
                pltpu.SemaphoreType.DMA((2,)),
                pltpu.SemaphoreType.DMA((2,)),
                pltpu.SemaphoreType.DMA((2,)),
                pltpu.SemaphoreType.REGULAR((2,)),
            ],
            compiler_params=pltpu.CompilerParams(collective_id=0, has_side_effects=True),
        )(*args)

    rep = P()
    tile = P("section", "rows", None, None)
    cache = P(None, "rows", None, None)
    return jax.shard_map(
        step,
        mesh=mesh,
        in_specs=(tile, cache, cache) + (rep,) * 8,
        out_specs=tile,
        check_vma=False,
    )
```
